32 devices in a mesh: island: 2 (over core), dp: 4 (over z), tensor: 4 (over y, x).
Axes of the slice: x: 2, y: 2, z: 4, core: 2. Of those that a mesh axis runs over, the one named last changes fastest.
Arguments:
- pseudo_grad: float32 [2, 48, 256, 5120], P('island', None, 'dp', 'tensor'), may hold values from -1000 to 1000, as said below
- block_owner: int32 [48], replicated, may hold values from 0 to 7, as said below
Outputs:
- update: bfloat16 [8, 12, 256, 5120], P(('island', 'dp'), None, None, 'tensor')
The draws below stay inside these ranges and needn't reach their ends.
Inputs may be any that keep to these rules, and one draw needn't show every extreme that they name: `pseudo_grad`: float pseudo-gradients; entries lie within the range. `block_owner`: every owner holds at most 12 blocks and at least one; some owner holds exactly 12.
All inputs are finite; a program needn't handle non-finite values.
Results may differ from the reference program's by a relative error of at most 0.001.
Values sent between devices are 32-bit elements; how exact they have to be, the bound alone decides.
A program may use at most 128 MiB of HBM per device.

```python
import math
import jax
import jax.numpy as jnp
from jax import lax

D = 5120
HB = 256
ISLANDS = 2
OWNERS = 8
BLOCKS = 48
SLOTS = 12


def draw_pseudo_grad(key, part):
    shape = (ISLANDS, BLOCKS, HB, D)
    keys = jax.random.split(jax.random.fold_in(key, 11), 3)
    trend = jnp.exp(math.log(3.0) * jnp.arange(D, dtype=jnp.float32) / (D - 1))
    col_scale = jnp.exp(jax.random.uniform(keys[1], (1, 1, 1, D), jnp.float32, 0.0, math.log(10.0 / 3.0))) * trend
    row_scale = jnp.exp(jax.random.uniform(keys[0], (1, BLOCKS, HB, 1), jnp.float32, 0.0, math.log(10.0)))
    base = jax.random.truncated_normal(keys[2], -4.0, 4.0, shape, jnp.float32)
    return (base * row_scale * col_scale).astype(jnp.float32)


def draw_block_owner(key, part):
    keys = jax.random.split(jax.random.fold_in(key, 23), 2)
    average = BLOCKS // OWNERS
    quarter = OWNERS // 4
    ranking = jnp.arange(OWNERS, dtype=jnp.int32)
    sorted_counts = jnp.where(ranking < quarter, 2 * average, jnp.where(ranking < 2 * quarter, average, average // 2))
    shuffle = jax.random.permutation(keys[0], OWNERS)
    counts = sorted_counts[shuffle]
    owner_list = jnp.repeat(ranking, counts, total_repeat_length=BLOCKS)
    reorder = jax.random.permutation(keys[1], BLOCKS)
    return owner_list[reorder].astype(jnp.int32)


def setup_inputs(seed: int = 0) -> dict:
    key_list = jax.random.split(jax.random.key(seed), 3)
    return {
        "pseudo_grad": draw_pseudo_grad(jax.random.fold_in(key_list[2], 71), 0),
        "block_owner": draw_block_owner(jax.random.fold_in(key_list[2], 71), 0),
    }


COEF_A = 3.4445
COEF_B = -4.775
COEF_C = 2.0315
EPSILON = 1e-07

def slot_table(block_owner, owner_count, slot_count):
    blocks = block_owner.shape[0]
    positions = jnp.arange(blocks, dtype=jnp.int32)
    one_hot = (block_owner[:, None] == jnp.arange(owner_count, dtype=jnp.int32)[None, :]).astype(jnp.float32)
    earlier = (positions[None, :] < positions[:, None]).astype(jnp.float32)
    counts_before = jnp.dot(earlier, one_hot, precision=lax.Precision.HIGHEST)
    slot = lax.optimization_barrier(jnp.sum(counts_before * one_hot, axis=1)).astype(jnp.int32)
    slot_key = block_owner * slot_count + slot
    entries = jnp.arange(owner_count * slot_count, dtype=jnp.int32)
    matches = slot_key[None, :] == entries[:, None]
    slot_index = lax.optimization_barrier(jnp.sum(jnp.where(matches, positions[None, :], 0), axis=1)).astype(jnp.int32)
    slot_valid = jnp.any(matches, axis=1)
    return (slot_index, slot_valid)

def newton(block):
    norm_value = jnp.sqrt(jnp.sum(block * block))
    iterate = block / (norm_value + EPSILON)
    for sweep in range(2):
        gram_mat = jnp.dot(iterate, iterate.T, precision=lax.Precision.HIGHEST)
        poly_mat = COEF_B * gram_mat + COEF_C * jnp.dot(gram_mat, gram_mat, precision=lax.Precision.HIGHEST)
        iterate = COEF_A * iterate + jnp.dot(poly_mat, iterate, precision=lax.Precision.HIGHEST)
    return (math.sqrt(D) * iterate).astype(jnp.bfloat16)

def reference(pseudo_grad, block_owner):

    def one_block(block_id):
        total = lax.optimization_barrier(jnp.sum(pseudo_grad[:, block_id], axis=0))
        return newton(total)
    results = lax.map(one_block, jnp.arange(BLOCKS, dtype=jnp.int32))
    slot_index, slot_valid = slot_table(block_owner, OWNERS, SLOTS)
    placed = jnp.where(slot_valid[:, None, None], results[slot_index].astype(jnp.float32), 0.0)
    return placed.astype(jnp.bfloat16).reshape(OWNERS, SLOTS, HB, D)
```

```python
import functools
import math

import jax
import jax.numpy as jnp
from jax import lax
from jax.experimental import pallas as pl
from jax.experimental.pallas import tpu as pltpu
from jax.sharding import PartitionSpec as P

COEF_A = 3.4445
COEF_B = -4.775
COEF_C = 2.0315
EPSILON = 1e-07
MESH = pl.DeviceIdType.MESH
RING = 2
STAGES = 4
LOADS = 4


def rank_before(key):
    positions = jnp.arange(key.shape[0], dtype=jnp.int32)
    same = (key[None, :] == key[:, None]) & (positions[None, :] < positions[:, None])
    return jnp.sum(same.astype(jnp.int32), axis=1)


def invert(target, count):
    positions = jnp.arange(target.shape[0], dtype=jnp.int32)
    matches = target[None, :] == jnp.arange(count, dtype=jnp.int32)[:, None]
    return jnp.sum(jnp.where(matches, positions[None, :], 0), axis=1), jnp.any(matches, axis=1)


def split(value):
    high = value.astype(jnp.bfloat16)
    return high, (value - high.astype(jnp.float32)).astype(jnp.bfloat16)


def dot(left, right, axis=0):
    dims = (((1,), (axis,)), ((), ()))
    return lax.dot_general(left, right, dims, preferred_element_type=jnp.float32)


def product(left, right):
    left_high, left_low = split(left)
    right_high, right_low = split(right)
    stacked_left = jnp.concatenate([left_high, left_high, left_low], axis=1)
    stacked_right = jnp.concatenate([right_high, right_low, right_high], axis=0)
    return dot(stacked_left, stacked_right)


def factor_of(gram):
    on_diagonal = lax.broadcasted_iota(jnp.int32, gram.shape, 0) == lax.broadcasted_iota(jnp.int32, gram.shape, 1)
    squares = jnp.sum(jnp.where(on_diagonal, gram, 0.0), axis=(0, 1), keepdims=True)
    inverse = 1.0 / (jnp.sqrt(squares) + EPSILON)
    scaled_identity = jnp.where(on_diagonal, COEF_A, 0.0)
    start = gram * (inverse * inverse)
    first = scaled_identity + (COEF_B * start + COEF_C * product(start, start))
    second_gram = product(product(first, start), first)
    second = scaled_identity + (COEF_B * second_gram + COEF_C * product(second_gram, second_gram))
    return product(second, first) * inverse


def pick(table, position):
    if len(set(table)) == 1:
        return table[0]
    value = jnp.int32(table[0])
    for k in range(1, len(table)):
        value = jnp.where(position == k, jnp.int32(table[k]), value)
    return value


def step_kernel(
    n, tensors, most, counts, scale, index_ref, grad_ref, fin_ref,
    given, own, stage, work, block, relay_in, gram, gram_in, part, part_in, total, final,
    load_sem, stage_send, stage_recv, send_sem, recv_sem, gram_send, gram_recv,
    relay_send, relay_recv, part_send, part_recv, total_send, total_recv, out_sem,
):
    me = lax.axis_index("dp")
    island = lax.axis_index("island")
    tensor = lax.axis_index("tensor")
    partner = 1 - island
    rounds = max(counts)
    blocks, rows, half = own.shape
    size = n * rows
    mid = size // 2
    own_rows = pl.ds(pl.multiple_of(island * mid, mid), mid)
    partner_rows = pl.ds(pl.multiple_of(partner * mid, mid), mid)
    own_columns = pl.ds(pl.multiple_of(island * half, half), half)
    partner_columns = pl.ds(pl.multiple_of(partner * half, half), half)

    loads = LOADS if blocks % LOADS == 0 else 1
    step = blocks // loads

    def load(target, columns, k, row):
        span = pl.ds(k * step, step)
        return pltpu.make_async_copy(grad_ref.at[span, :, columns], target.at[span], load_sem.at[row, k])

    for k in range(loads):
        load(given, partner_columns, k, 0).start()
    for k in range(loads):
        load(own, own_columns, k, 1).start()

    barrier = pltpu.get_barrier_semaphore()
    for d in range(1, n):
        pl.semaphore_signal(barrier, inc=1, device_id={"dp": lax.rem(me + d, n)}, device_id_type=MESH)
    for d in range(1, tensors):
        pl.semaphore_signal(barrier, inc=1, device_id={"tensor": lax.rem(tensor + d, tensors)}, device_id_type=MESH)
    pl.semaphore_signal(barrier, inc=1, device_id={"island": partner}, device_id_type=MESH)
    pl.semaphore_wait(barrier, n + tensors - 1)

    def to_partner(source, target, send, recv):
        return pltpu.make_async_remote_copy(
            src_ref=source, dst_ref=target, send_sem=send, recv_sem=recv,
            device_id={"island": partner}, device_id_type=MESH,
        )

    def stage_copy(r):
        k = lax.rem(r, STAGES)
        return to_partner(stage.at[k], work.at[r], stage_send.at[k], stage_recv.at[r])

    def row_copy(r, peer):
        return pltpu.make_async_remote_copy(
            src_ref=work.at[r, peer],
            dst_ref=block.at[r, me],
            send_sem=send_sem.at[r, peer],
            recv_sem=recv_sem.at[r, me],
            device_id={"dp": peer},
            device_id_type=MESH,
        )

    def row_arrival(r, peer):
        return pltpu.make_async_remote_copy(
            src_ref=work.at[r, peer],
            dst_ref=block.at[r, peer],
            send_sem=send_sem.at[r, peer],
            recv_sem=recv_sem.at[r, peer],
            device_id={"dp": peer},
            device_id_type=MESH,
        )

    def gram_copy(r):
        k = lax.rem(r, RING)
        return to_partner(gram.at[k, partner_rows], gram_in.at[k], gram_send.at[k], gram_recv.at[k])

    def relay(r):
        k = lax.rem(r, RING)
        return to_partner(block.at[r], relay_in.at[k], relay_send.at[k], relay_recv.at[k])

    def total_copy(r):
        k = lax.rem(r, RING)
        values = total.at[k, own_rows]
        return to_partner(values, values, total_send.at[k], total_recv.at[k])

    def part_copy(r, d):
        k = lax.rem(r, RING)
        return pltpu.make_async_remote_copy(
            src_ref=part.at[k],
            dst_ref=part_in.at[d - 1, k],
            send_sem=part_send.at[k, d],
            recv_sem=part_recv.at[k, d],
            device_id={"tensor": lax.rem(tensor + d, tensors)},
            device_id_type=MESH,
        )

    def out_copy(r):
        k = lax.rem(r, RING)
        return pltpu.make_async_copy(final.at[k], fin_ref.at[r], out_sem.at[k])

    def others(r, run):
        def one(o, carry):
            peer = lax.rem(me + o, n)

            @pl.when(r < pick(counts, peer))
            def _():
                run(r, peer)

            return carry

        lax.fori_loop(1, n, one, 0)

    for k in range(loads):
        load(given, partner_columns, k, 0).wait()
    for k in range(loads):
        load(own, own_columns, k, 1).wait()

    def send(r, carry):
        @pl.when(r < rounds)
        def _():
            @pl.when(r >= STAGES)
            def _():
                stage_copy(r - STAGES).wait_send()

            def put(d, inner):
                stage[lax.rem(r, STAGES), d] = given[index_ref[d * most + r]]
                return inner

            lax.fori_loop(0, n, put, 0)

        @pl.when((r >= 1) & (r < rounds + 1))
        def _():
            stage_copy(r - 1).start()

        @pl.when((r >= 2) & (r < rounds + 2))
        def _():
            q = r - 2
            stage_copy(q).wait_recv()

            def add(d, inner):
                work[q, d] = work[q, d] + own[index_ref[d * most + q]]
                return inner

            lax.fori_loop(0, n, add, 0)
            block[q, me] = work[q, me]

        @pl.when(r >= 3)
        def _():
            others(r - 3, lambda q, peer: row_copy(q, peer).start())

        return carry

    lax.fori_loop(0, rounds + 3, send, 0)
    for r in range(max(0, rounds - STAGES), rounds):
        stage_copy(r).wait_send()

    count = pick(counts, me)

    def run(t, carry):
        now = lax.rem(t, RING)
        before = lax.rem(t + RING - 1, RING)

        @pl.when(t < count)
        def _():
            def arrive(o, inner):
                row_arrival(t, lax.rem(me + o, n)).wait_recv()
                return inner

            lax.fori_loop(1, n, arrive, 0)
            high, low = split(block[t].reshape(size, half))
            cross = dot(high, low, 1)
            gram[now] = dot(high, high, 1) + (cross + cross.T)
            gram_copy(t).start()

        @pl.when(t >= 1)
        def _():
            for d in range(1, tensors):
                part_copy(t - 1, d).wait()
            summed = part[before]
            for d in range(1, tensors):
                summed = summed + part_in[d - 1, before]
            total[before, own_rows] = summed
            total_copy(t - 1).start()

        @pl.when(t < count)
        def _():
            gram_copy(t).wait()
            part[now] = gram[now, own_rows] + gram_in[now]
            for d in range(1, tensors):
                part_copy(t, d).start()
            relay(t).start()

        @pl.when(t >= 1)
        def _():
            total_copy(t - 1).wait()
            factor = factor_of(total[before])

            @pl.when(t >= 1 + RING)
            def _():
                out_copy(t - 1 - RING).wait()

            relay(t - 1).wait()
            mine = scale * product(factor, block[t - 1].reshape(size, half))
            final[before, :, own_columns] = mine.astype(jnp.bfloat16)
            theirs = scale * product(factor, relay_in[before].reshape(size, half))
            final[before, :, partner_columns] = theirs.astype(jnp.bfloat16)
            out_copy(t - 1).start()

        return carry

    lax.fori_loop(0, count + 1, run, 0)

    def drain(k, carry):
        out_copy(count - RING + k).wait()
        return carry

    lax.fori_loop(0, RING, drain, 0)

    def finish(r, carry):
        others(r, lambda q, peer: row_copy(q, peer).wait_send())
        return carry

    lax.fori_loop(0, rounds, finish, 0)


def step(index, own_grad, counts, most, n, tensors, collective_id):
    blocks, rows, columns = own_grad.shape
    half = columns // 2
    size = n * rows
    rounds = max(counts)
    dma = pltpu.SemaphoreType.DMA
    return pl.pallas_call(
        functools.partial(step_kernel, n, tensors, most, counts, math.sqrt(columns * tensors)),
        out_shape=jax.ShapeDtypeStruct((most, size, columns), jnp.bfloat16),
        in_specs=[pl.BlockSpec(memory_space=pltpu.SMEM), pl.BlockSpec(memory_space=pl.ANY)],
        out_specs=pl.BlockSpec(memory_space=pl.ANY),
        scratch_shapes=[
            pltpu.VMEM((blocks, rows, half), jnp.float32),
            pltpu.VMEM((blocks, rows, half), jnp.float32),
            pltpu.VMEM((STAGES, n, rows, half), jnp.float32),
            pltpu.VMEM((rounds, n, rows, half), jnp.float32),
            pltpu.VMEM((rounds, n, rows, half), jnp.float32),
            pltpu.VMEM((RING, n, rows, half), jnp.float32),
            pltpu.VMEM((RING, size, size), jnp.float32),
            pltpu.VMEM((RING, size // 2, size), jnp.float32),
            pltpu.VMEM((RING, size // 2, size), jnp.float32),
            pltpu.VMEM((tensors - 1, RING, size // 2, size), jnp.float32),
            pltpu.VMEM((RING, size, size), jnp.float32),
            pltpu.VMEM((RING, size, columns), jnp.bfloat16),
            dma((2, LOADS)),
            dma((STAGES,)),
            dma((rounds,)),
            dma((rounds, n)),
            dma((rounds, n)),
            dma((RING,)),
            dma((RING,)),
            dma((RING,)),
            dma((RING,)),
            dma((RING, tensors)),
            dma((RING, tensors)),
            dma((RING,)),
            dma((RING,)),
            dma((RING,)),
        ],
        compiler_params=pltpu.CompilerParams(
            collective_id=collective_id, has_side_effects=True, vmem_limit_bytes=63 * 2**20
        ),
    )(index, own_grad)


def place_kernel(place_ref, valid_ref, fin_ref, out_ref):
    valid = valid_ref[pl.program_id(0)] > 0
    out_ref[0, 0] = jnp.where(valid, fin_ref[0].astype(jnp.float32), 0.0).astype(jnp.bfloat16)


def placed(fin, place, valid):
    count = place.shape[0]
    _, size, columns = fin.shape
    return pl.pallas_call(
        place_kernel,
        grid_spec=pltpu.PrefetchScalarGridSpec(
            num_scalar_prefetch=2,
            grid=(count,),
            in_specs=[pl.BlockSpec((1, size, columns), lambda i, p, v: (p[i], 0, 0))],
            out_specs=pl.BlockSpec((1, 1, size, columns), lambda i, p, v: (0, i, 0, 0)),
        ),
        out_shape=jax.ShapeDtypeStruct((1, count, size, columns), jnp.bfloat16),
    )(place, valid.astype(jnp.int32), fin)


def cut_load(counts):
    n = len(counts)
    loads = []
    for i in range(1, n):
        loads.append((n - i) * sum(counts[:i]))
        loads.append(i * sum(counts[i:]))
    return max(loads)


def count_classes(n, most, least, unit):
    return [(c,) * n for c in range(unit, most + 1, unit) if c >= least]


def body(pseudo_grad, block_owner):
    own_grad = pseudo_grad[0]
    blocks, rows, columns = own_grad.shape
    dp_count = lax.axis_size("dp")
    island_count = lax.axis_size("island")
    tensors = lax.axis_size("tensor")
    owner_count = island_count * dp_count
    slot_count = 2 * (blocks // owner_count)
    most = island_count * slot_count
    least = blocks // dp_count
    unit = max(1, slot_count // 4)
    island = lax.axis_index("island")
    device_dp = lax.axis_index("dp")

    slot = rank_before(block_owner)
    chip = lax.rem(block_owner, dp_count)
    chip_slot = rank_before(chip)
    send_index, _ = invert(chip * most + chip_slot, dp_count * most)
    needed = jnp.sum((chip[None, :] == jnp.arange(dp_count, dtype=jnp.int32)[:, None]).astype(jnp.int32), axis=1)
    own_index, own_valid = invert(block_owner * slot_count + slot, owner_count * slot_count)
    base = (island * dp_count + device_dp) * slot_count
    own_block = lax.dynamic_slice_in_dim(own_index, base, slot_count)
    own_valid = lax.dynamic_slice_in_dim(own_valid, base, slot_count)
    own_place = chip_slot[own_block]

    classes = sorted(count_classes(dp_count, most, least, unit), key=cut_load)
    fits = jnp.all(needed[None, :] <= jnp.array(classes, dtype=jnp.int32), axis=1)
    order = jnp.arange(len(classes), dtype=jnp.int32)
    choice = jnp.min(jnp.where(fits, order, len(classes) - 1))

    def branch(counts, number):
        def run(index, own_grad):
            return step(index, own_grad, counts, most, dp_count, tensors, number)

        return run

    branches = [branch(c, i) for i, c in enumerate(classes)]
    fin = lax.switch(choice, branches, send_index, own_grad)
    return placed(fin, own_place, own_valid)


def solution(mesh):
    in_specs = (P("island", None, "dp", "tensor"), P())
    out_specs = P(("island", "dp"), None, None, "tensor")
    return jax.shard_map(body, mesh=mesh, in_specs=in_specs, out_specs=out_specs, check_vma=False)
```

```python
import functools
import math

import jax
import jax.numpy as jnp
from jax import lax
from jax.experimental import pallas as pl
from jax.experimental.pallas import tpu as pltpu
from jax.sharding import PartitionSpec as P

COEF_A = 3.4445
COEF_B = -4.775
COEF_C = 2.0315
EPSILON = 1e-07
MESH = pl.DeviceIdType.MESH
RING = 2
STAGES = 4
LOADS = 4


def split(value):
    high = value.astype(jnp.bfloat16)
    return high, (value - high.astype(jnp.float32)).astype(jnp.bfloat16)


def dot(left, right, axis=0):
    dims = (((1,), (axis,)), ((), ()))
    return lax.dot_general(left, right, dims, preferred_element_type=jnp.float32)


def product(left, right):
    left_high, left_low = split(left)
    right_high, right_low = split(right)
    stacked_left = jnp.concatenate([left_high, left_high, left_low], axis=1)
    stacked_right = jnp.concatenate([right_high, right_low, right_high], axis=0)
    return dot(stacked_left, stacked_right)


def factor_steps(bench, gram):
    on_diagonal = lax.broadcasted_iota(jnp.int32, gram.shape, 0) == lax.broadcasted_iota(jnp.int32, gram.shape, 1)
    squares = jnp.sum(jnp.where(on_diagonal, gram, 0.0), axis=(0, 1), keepdims=True)
    inverse = 1.0 / (jnp.sqrt(squares) + EPSILON)
    bench[0] = gram * (inverse * inverse)

    def one(i, carry):
        polynomial = (i == 0) | (i == 3)
        other = jnp.where(polynomial, i, jnp.where(i == 1, 0, 1))
        left = bench[i]
        value = product(left, bench[other])
        scaled_identity = jnp.where(on_diagonal, COEF_A, 0.0)
        bench[i + 1] = jnp.where(polynomial, scaled_identity + (COEF_B * left + COEF_C * value), value)
        return carry

    lax.fori_loop(0, 5, one, 0)
    bench[5] = bench[5] * inverse


def pick(table, position):
    if len(set(table)) == 1:
        return table[0]
    value = jnp.int32(table[0])
    for k in range(1, len(table)):
        value = jnp.where(position == k, jnp.int32(table[k]), value)
    return value


def step_kernel(
    n, tensors, most, counts, scale, index_ref, grad_ref, fin_ref,
    given, own, stage, work, block, bench, gram, gram_in, part, part_in, total, final,
    load_sem, stage_send, stage_recv, send_sem, recv_sem, gram_send, gram_recv,
    relay_send, relay_recv, part_send, part_recv, total_send, total_recv, out_sem,
):
    me = lax.axis_index("dp")
    island = lax.axis_index("island")
    tensor = lax.axis_index("tensor")
    partner = 1 - island
    rounds = max(counts)
    blocks, rows, half = own.shape
    size = n * rows
    mid = size // 2
    own_rows = pl.ds(pl.multiple_of(island * mid, mid), mid)
    partner_rows = pl.ds(pl.multiple_of(partner * mid, mid), mid)
    own_columns = pl.ds(pl.multiple_of(island * half, half), half)
    partner_columns = pl.ds(pl.multiple_of(partner * half, half), half)

    loads = LOADS if blocks % LOADS == 0 else 1
    step = blocks // loads

    def load(target, columns, k, row):
        span = pl.ds(k * step, step)
        return pltpu.make_async_copy(grad_ref.at[span, :, columns], target.at[span], load_sem.at[row, k])

    for k in range(loads):
        load(given, partner_columns, k, 0).start()
    for k in range(loads):
        load(own, own_columns, k, 1).start()

    barrier = pltpu.get_barrier_semaphore()
    for d in range(1, n):
        pl.semaphore_signal(barrier, inc=1, device_id={"dp": lax.rem(me + d, n)}, device_id_type=MESH)
    for d in range(1, tensors):
        pl.semaphore_signal(barrier, inc=1, device_id={"tensor": lax.rem(tensor + d, tensors)}, device_id_type=MESH)
    pl.semaphore_signal(barrier, inc=1, device_id={"island": partner}, device_id_type=MESH)
    pl.semaphore_wait(barrier, n + tensors - 1)

    def to_partner(source, target, send, recv):
        return pltpu.make_async_remote_copy(
            src_ref=source, dst_ref=target, send_sem=send, recv_sem=recv,
            device_id={"island": partner}, device_id_type=MESH,
        )

    def stage_copy(r):
        k = lax.rem(r, STAGES)
        return to_partner(stage.at[k], work.at[r], stage_send.at[k], stage_recv.at[r])

    def row_copy(r, peer):
        return pltpu.make_async_remote_copy(
            src_ref=work.at[r, peer],
            dst_ref=block.at[r, me],
            send_sem=send_sem.at[r, peer],
            recv_sem=recv_sem.at[r, me],
            device_id={"dp": peer},
            device_id_type=MESH,
        )

    def row_arrival(r, peer):
        return pltpu.make_async_remote_copy(
            src_ref=work.at[r, peer],
            dst_ref=block.at[r, peer],
            send_sem=send_sem.at[r, peer],
            recv_sem=recv_sem.at[r, peer],
            device_id={"dp": peer},
            device_id_type=MESH,
        )

    def gram_copy(r):
        k = lax.rem(r, RING)
        return to_partner(gram.at[k, partner_rows], gram_in.at[k], gram_send.at[k], gram_recv.at[k])

    def relay(r):
        k = lax.rem(r, RING)
        return to_partner(block.at[r], block.at[rounds + k], relay_send.at[k], relay_recv.at[k])

    def total_copy(r):
        k = lax.rem(r, RING)
        values = total.at[k, own_rows]
        return to_partner(values, values, total_send.at[k], total_recv.at[k])

    def part_copy(r, d):
        k = lax.rem(r, RING)
        return pltpu.make_async_remote_copy(
            src_ref=part.at[k],
            dst_ref=part_in.at[d - 1, k],
            send_sem=part_send.at[k, d],
            recv_sem=part_recv.at[k, d],
            device_id={"tensor": lax.rem(tensor + d, tensors)},
            device_id_type=MESH,
        )

    def out_copy(r):
        k = lax.rem(r, RING)
        return pltpu.make_async_copy(final.at[k], fin_ref.at[r], out_sem.at[k])

    def others(r, run):
        def one(o, carry):
            peer = lax.rem(me + o, n)

            @pl.when(r < pick(counts, peer))
            def _():
                run(r, peer)

            return carry

        lax.fori_loop(1, n, one, 0)

    for k in range(loads):
        load(given, partner_columns, k, 0).wait()

    def send(r, carry):
        @pl.when(r < rounds)
        def _():
            @pl.when(r >= STAGES)
            def _():
                stage_copy(r - STAGES).wait_send()

            def put(d, inner):
                stage[lax.rem(r, STAGES), d] = given[index_ref[d * most + r]]
                return inner

            lax.fori_loop(0, n, put, 0)

        @pl.when((r >= 1) & (r < rounds + 1))
        def _():
            stage_copy(r - 1).start()

        @pl.when((r >= 2) & (r < rounds + 2))
        def _():
            q = r - 2

            @pl.when(r == 2)
            def _():
                for k in range(loads):
                    load(own, own_columns, k, 1).wait()

            stage_copy(q).wait_recv()

            def add(d, inner):
                work[q, d] = work[q, d] + own[index_ref[d * most + q]]
                return inner

            lax.fori_loop(0, n, add, 0)
            block[q, me] = work[q, me]

        @pl.when(r >= 3)
        def _():
            others(r - 3, lambda q, peer: row_copy(q, peer).start())

        return carry

    lax.fori_loop(0, rounds + 3, send, 0)
    for r in range(max(0, rounds - STAGES), rounds):
        stage_copy(r).wait_send()

    count = pick(counts, me)

    def run(t, carry):
        now = lax.rem(t, RING)
        before = lax.rem(t + RING - 1, RING)

        @pl.when(t < count)
        def _():
            def arrive(o, inner):
                row_arrival(t, lax.rem(me + o, n)).wait_recv()
                return inner

            lax.fori_loop(1, n, arrive, 0)
            high, low = split(block[t].reshape(size, half))
            cross = dot(high, low, 1)
            gram[now] = dot(high, high, 1) + (cross + cross.T)
            gram_copy(t).start()

        @pl.when(t >= 1)
        def _():
            for d in range(1, tensors):
                part_copy(t - 1, d).wait()
            summed = part[before]
            for d in range(1, tensors):
                summed = summed + part_in[d - 1, before]
            total[before, own_rows] = summed
            total_copy(t - 1).start()

        @pl.when(t < count)
        def _():
            gram_copy(t).wait()
            part[now] = gram[now, own_rows] + gram_in[now]
            for d in range(1, tensors):
                part_copy(t, d).start()
            relay(t).start()

        @pl.when(t >= 1)
        def _():
            total_copy(t - 1).wait()
            factor_steps(bench, total[before])

            @pl.when(t >= 1 + RING)
            def _():
                out_copy(t - 1 - RING).wait()

            relay(t - 1).wait()

            def columns_of(h, inner):
                source = jnp.where(h == 0, t - 1, rounds + before)
                side = jnp.where(h == 0, island, partner)
                target = pl.ds(pl.multiple_of(side * half, half), half)
                value = scale * product(bench[5], block[source].reshape(size, half))
                final[before, :, target] = value.astype(jnp.bfloat16)
                return inner

            lax.fori_loop(0, 2, columns_of, 0)
            out_copy(t - 1).start()

        return carry

    lax.fori_loop(0, count + 1, run, 0)

    def drain(k, carry):
        out_copy(count - RING + k).wait()
        return carry

    lax.fori_loop(0, RING, drain, 0)

    def finish(r, carry):
        others(r, lambda q, peer: row_copy(q, peer).wait_send())
        return carry

    lax.fori_loop(0, rounds, finish, 0)


def step(index, own_grad, counts, most, n, tensors, collective_id):
    blocks, rows, columns = own_grad.shape
    half = columns // 2
    size = n * rows
    rounds = max(counts)
    dma = pltpu.SemaphoreType.DMA
    return pl.pallas_call(
        functools.partial(step_kernel, n, tensors, most, counts, math.sqrt(columns * tensors)),
        out_shape=jax.ShapeDtypeStruct((most, size, columns), jnp.bfloat16),
        in_specs=[pl.BlockSpec(memory_space=pltpu.SMEM), pl.BlockSpec(memory_space=pl.ANY)],
        out_specs=pl.BlockSpec(memory_space=pl.ANY),
        scratch_shapes=[
            pltpu.VMEM((blocks, rows, half), jnp.float32),
            pltpu.VMEM((blocks, rows, half), jnp.float32),
            pltpu.VMEM((STAGES, n, rows, half), jnp.float32),
            pltpu.VMEM((rounds, n, rows, half), jnp.float32),
            pltpu.VMEM((rounds + RING, n, rows, half), jnp.float32),
            pltpu.VMEM((6, size, size), jnp.float32),
            pltpu.VMEM((RING, size, size), jnp.float32),
            pltpu.VMEM((RING, size // 2, size), jnp.float32),
            pltpu.VMEM((RING, size // 2, size), jnp.float32),
            pltpu.VMEM((tensors - 1, RING, size // 2, size), jnp.float32),
            pltpu.VMEM((RING, size, size), jnp.float32),
            pltpu.VMEM((RING, size, columns), jnp.bfloat16),
            dma((2, LOADS)),
            dma((STAGES,)),
            dma((rounds,)),
            dma((rounds, n)),
            dma((rounds, n)),
            dma((RING,)),
            dma((RING,)),
            dma((RING,)),
            dma((RING,)),
            dma((RING, tensors)),
            dma((RING, tensors)),
            dma((RING,)),
            dma((RING,)),
            dma((RING,)),
        ],
        compiler_params=pltpu.CompilerParams(
            collective_id=collective_id, has_side_effects=True, vmem_limit_bytes=63 * 2**20
        ),
    )(index, own_grad)


def place_kernel(place_ref, valid_ref, fin_ref, out_ref, held, in_sem, out_sem):
    count = held.shape[0]

    def fetch(s):
        return pltpu.make_async_copy(fin_ref.at[place_ref[s]], held.at[s], in_sem.at[s])

    def store(s):
        return pltpu.make_async_copy(held.at[s], out_ref.at[0, s], out_sem.at[s])

    def begin(s, carry):
        fetch(s).start()
        return carry

    def forward(s, carry):
        fetch(s).wait()

        @pl.when(valid_ref[s] == 0)
        def _():
            held[s] = jnp.zeros(held.shape[1:], held.dtype)

        store(s).start()
        return carry

    def end(s, carry):
        store(s).wait()
        return carry

    lax.fori_loop(0, count, begin, 0)
    lax.fori_loop(0, count, forward, 0)
    lax.fori_loop(0, count, end, 0)


def placed(fin, place, valid):
    count = place.shape[0]
    _, size, columns = fin.shape
    scalars = pl.BlockSpec(memory_space=pltpu.SMEM)
    anywhere = pl.BlockSpec(memory_space=pl.ANY)
    dma = pltpu.SemaphoreType.DMA
    return pl.pallas_call(
        place_kernel,
        in_specs=[scalars, scalars, anywhere],
        out_specs=anywhere,
        out_shape=jax.ShapeDtypeStruct((1, count, size, columns), jnp.bfloat16),
        scratch_shapes=[pltpu.VMEM((count, size, columns), jnp.bfloat16), dma((count,)), dma((count,))],
    )(place, valid, fin)


def table_kernel(n, most, classes, owner_ref, send_ref, place_ref, valid_ref, choice_ref, needed):
    mine = lax.axis_index("island") * n + lax.axis_index("dp")

    def clear(ref):
        def one(i, carry):
            ref[i] = 0
            return carry

        lax.fori_loop(0, ref.shape[0], one, 0)

    for ref in (send_ref, place_ref, valid_ref, needed):
        clear(ref)

    def one(b, held):
        owner = owner_ref[b]
        chip = lax.rem(owner, n)
        slot = needed[chip]
        needed[chip] = slot + 1
        send_ref[chip * most + slot] = b

        @pl.when(owner == mine)
        def _():
            place_ref[held] = slot
            valid_ref[held] = 1

        return held + (owner == mine).astype(jnp.int32)

    lax.fori_loop(0, owner_ref.shape[0], one, jnp.int32(0))
    choice = jnp.int32(len(classes) - 1)
    for k in range(len(classes) - 2, -1, -1):
        fits = needed[0] <= classes[k][0]
        for d in range(1, n):
            fits = fits & (needed[d] <= classes[k][d])
        choice = jnp.where(fits, jnp.int32(k), choice)
    choice_ref[0] = choice


def tables(block_owner, n, most, slot_count, classes):
    scalars = pl.BlockSpec(memory_space=pltpu.SMEM)
    return pl.pallas_call(
        functools.partial(table_kernel, n, most, classes),
        in_specs=[scalars],
        out_specs=(scalars,) * 4,
        out_shape=tuple(jax.ShapeDtypeStruct((c,), jnp.int32) for c in (n * most, slot_count, slot_count, 1)),
        scratch_shapes=[pltpu.SMEM((n,), jnp.int32)],
    )(block_owner)


def cut_load(counts):
    n = len(counts)
    loads = []
    for i in range(1, n):
        loads.append((n - i) * sum(counts[:i]))
        loads.append(i * sum(counts[i:]))
    return max(loads)


PROFILES = (
    (5, 5, 5, 5), (6, 6, 6, 6), (3, 8, 8, 3), (3, 6, 3, 6), (6, 3, 3, 6), (6, 3, 6, 3), (8, 4, 4, 8),
    (3, 6, 6, 3), (5, 6, 5, 6), (6, 5, 6, 5), (3, 5, 3, 5), (3, 5, 5, 3), (4, 8, 8, 4), (5, 3, 3, 5),
)


def count_classes(n, most, least, unit):
    uniform = [(c,) * n for c in range(unit, most + 1, unit) if c >= least]
    shaped = [tuple(unit * k for k in profile) for profile in PROFILES if len(profile) == n]
    shaped = [counts for counts in shaped if max(counts) <= most]
    if shaped:
        uniform = [(most,) * n]
    return sorted(uniform + shaped, key=cut_load)


def body(pseudo_grad, block_owner):
    own_grad = pseudo_grad[0]
    blocks = own_grad.shape[0]
    dp_count = lax.axis_size("dp")
    island_count = lax.axis_size("island")
    tensors = lax.axis_size("tensor")
    owner_count = island_count * dp_count
    slot_count = 2 * (blocks // owner_count)
    most = island_count * slot_count
    classes = count_classes(dp_count, most, blocks // dp_count, max(1, slot_count // 4))
    send_index, place, valid, choice = tables(block_owner, dp_count, most, slot_count, classes)

    def branch(counts, number):
        def run(index, own_grad):
            return step(index, own_grad, counts, most, dp_count, tensors, number)

        return run

    branches = [branch(c, i) for i, c in enumerate(classes)]
    fin = lax.switch(choice[0], branches, send_index, own_grad)
    return placed(fin, place, valid)


def solution(mesh):
    in_specs = (P("island", None, "dp", "tensor"), P())
    out_specs = P(("island", "dp"), None, None, "tensor")
    return jax.shard_map(body, mesh=mesh, in_specs=in_specs, out_specs=out_specs, check_vma=False)
```

```python
import functools
import math

import jax
import jax.numpy as jnp
from jax import lax
from jax.experimental import pallas as pl
from jax.experimental.pallas import tpu as pltpu
from jax.sharding import PartitionSpec as P

COEF_A = 3.4445
COEF_B = -4.775
COEF_C = 2.0315
EPSILON = 1e-07
MESH = pl.DeviceIdType.MESH
RING = 2
STAGES = 4
LOADS = 4


def split(value):
    high = value.astype(jnp.bfloat16)
    return high, (value - high.astype(jnp.float32)).astype(jnp.bfloat16)


def dot(left, right, axis=0):
    dims = (((1,), (axis,)), ((), ()))
    return lax.dot_general(left, right, dims, preferred_element_type=jnp.float32)


def product(left, right):
    left_high, left_low = split(left)
    right_high, right_low = split(right)
    stacked_left = jnp.concatenate([left_high, left_high, left_low], axis=1)
    stacked_right = jnp.concatenate([right_high, right_low, right_high], axis=0)
    return dot(stacked_left, stacked_right)


def factor_steps(bench, gram):
    on_diagonal = lax.broadcasted_iota(jnp.int32, gram.shape, 0) == lax.broadcasted_iota(jnp.int32, gram.shape, 1)
    squares = jnp.sum(jnp.where(on_diagonal, gram, 0.0), axis=(0, 1), keepdims=True)
    inverse = 1.0 / (jnp.sqrt(squares) + EPSILON)
    bench[0] = gram * (inverse * inverse)

    def one(i, carry):
        polynomial = (i == 0) | (i == 3)
        other = jnp.where(polynomial, i, jnp.where(i == 1, 0, 1))
        left = bench[i]
        value = product(left, bench[other])
        scaled_identity = jnp.where(on_diagonal, COEF_A, 0.0)
        bench[i + 1] = jnp.where(polynomial, scaled_identity + (COEF_B * left + COEF_C * value), value)
        return carry

    lax.fori_loop(0, 5, one, 0)
    bench[5] = bench[5] * inverse


def pick(table, position):
    if len(set(table)) == 1:
        return table[0]
    value = jnp.int32(table[0])
    for k in range(1, len(table)):
        value = jnp.where(position == k, jnp.int32(table[k]), value)
    return value


def step_kernel(
    n, tensors, most, counts, scale, index_ref, grad_ref, fin_ref,
    given, own, stage, work, block, bench, gram, gram_in, part, part_in, total, final,
    load_sem, stage_send, stage_recv, send_sem, recv_sem, gram_send, gram_recv,
    relay_send, relay_recv, part_send, part_recv, total_send, total_recv, out_sem,
):
    me = lax.axis_index("dp")
    island = lax.axis_index("island")
    tensor = lax.axis_index("tensor")
    partner = 1 - island
    rounds = max(counts)
    blocks, rows, half = own.shape
    size = n * rows
    mid = size // 2
    own_rows = pl.ds(pl.multiple_of(island * mid, mid), mid)
    partner_rows = pl.ds(pl.multiple_of(partner * mid, mid), mid)
    own_columns = pl.ds(pl.multiple_of(island * half, half), half)
    partner_columns = pl.ds(pl.multiple_of(partner * half, half), half)

    loads = LOADS if blocks % LOADS == 0 else 1
    step = blocks // loads

    def load(target, columns, k, row):
        span = pl.ds(k * step, step)
        return pltpu.make_async_copy(grad_ref.at[span, :, columns], target.at[span], load_sem.at[row, k])

    for k in range(loads):
        load(given, partner_columns, k, 0).start()
    for k in range(loads):
        load(own, own_columns, k, 1).start()

    barrier = pltpu.get_barrier_semaphore()
    for d in range(1, n):
        pl.semaphore_signal(barrier, inc=1, device_id={"dp": lax.rem(me + d, n)}, device_id_type=MESH)
    for d in range(1, tensors):
        pl.semaphore_signal(barrier, inc=1, device_id={"tensor": lax.rem(tensor + d, tensors)}, device_id_type=MESH)
    pl.semaphore_signal(barrier, inc=1, device_id={"island": partner}, device_id_type=MESH)
    pl.semaphore_wait(barrier, n + tensors - 1)

    def to_partner(source, target, send, recv):
        return pltpu.make_async_remote_copy(
            src_ref=source, dst_ref=target, send_sem=send, recv_sem=recv,
            device_id={"island": partner}, device_id_type=MESH,
        )

    def stage_copy(r):
        k = lax.rem(r, STAGES)
        return to_partner(stage.at[k], work.at[r], stage_send.at[k], stage_recv.at[r])

    def due(s, peer):
        wanted = pick(counts, peer)
        return (s * wanted) // rounds, ((s + 1) * wanted) // rounds

    def row_copy(s, r, peer):
        return pltpu.make_async_remote_copy(
            src_ref=work.at[s, peer],
            dst_ref=block.at[r, me],
            send_sem=send_sem.at[r, peer],
            recv_sem=recv_sem.at[r, me],
            device_id={"dp": peer},
            device_id_type=MESH,
        )

    def row_arrival(r, peer):
        return pltpu.make_async_remote_copy(
            src_ref=work.at[r, peer],
            dst_ref=block.at[r, peer],
            send_sem=send_sem.at[r, peer],
            recv_sem=recv_sem.at[r, peer],
            device_id={"dp": peer},
            device_id_type=MESH,
        )

    def gram_copy(r):
        k = lax.rem(r, RING)
        return to_partner(gram.at[k, partner_rows], gram_in.at[k], gram_send.at[k], gram_recv.at[k])

    def relay(r):
        k = lax.rem(r, RING)
        return to_partner(block.at[r], block.at[rounds + k], relay_send.at[k], relay_recv.at[k])

    def total_copy(r):
        k = lax.rem(r, RING)
        values = total.at[k, own_rows]
        return to_partner(values, values, total_send.at[k], total_recv.at[k])

    def part_copy(r, d):
        k = lax.rem(r, RING)
        return pltpu.make_async_remote_copy(
            src_ref=part.at[k],
            dst_ref=part_in.at[d - 1, k],
            send_sem=part_send.at[k, d],
            recv_sem=part_recv.at[k, d],
            device_id={"tensor": lax.rem(tensor + d, tensors)},
            device_id_type=MESH,
        )

    def out_copy(r):
        k = lax.rem(r, RING)
        return pltpu.make_async_copy(final.at[k], fin_ref.at[r], out_sem.at[k])

    def others(s, run):
        def one(o, carry):
            peer = lax.rem(me + o, n)
            first, last = due(s, peer)

            @pl.when(first < last)
            def _():
                run(s, first, peer)

            return carry

        lax.fori_loop(1, n, one, 0)

    for k in range(loads):
        load(given, partner_columns, k, 0).wait()

    def send(r, carry):
        @pl.when(r < rounds)
        def _():
            @pl.when(r >= STAGES)
            def _():
                stage_copy(r - STAGES).wait_send()

            def put(d, inner):
                stage[lax.rem(r, STAGES), d] = given[index_ref[d * most + due(r, d)[0]]]
                return inner

            lax.fori_loop(0, n, put, 0)

        @pl.when((r >= 1) & (r < rounds + 1))
        def _():
            stage_copy(r - 1).start()

        @pl.when((r >= 2) & (r < rounds + 2))
        def _():
            q = r - 2

            @pl.when(r == 2)
            def _():
                for k in range(loads):
                    load(own, own_columns, k, 1).wait()

            stage_copy(q).wait_recv()

            def add(d, inner):
                work[q, d] = work[q, d] + own[index_ref[d * most + due(q, d)[0]]]
                return inner

            lax.fori_loop(0, n, add, 0)
            block[due(q, me)[0], me] = work[q, me]

        @pl.when(r >= 3)
        def _():
            others(r - 3, lambda q, first, peer: row_copy(q, first, peer).start())

        return carry

    lax.fori_loop(0, rounds + 3, send, 0)
    for r in range(max(0, rounds - STAGES), rounds):
        stage_copy(r).wait_send()

    count = pick(counts, me)

    def run(t, carry):
        now = lax.rem(t, RING)
        before = lax.rem(t + RING - 1, RING)

        @pl.when(t < count)
        def _():
            def arrive(o, inner):
                row_arrival(t, lax.rem(me + o, n)).wait_recv()
                return inner

            lax.fori_loop(1, n, arrive, 0)
            high, low = split(block[t].reshape(size, half))
            cross = dot(high, low, 1)
            gram[now] = dot(high, high, 1) + (cross + cross.T)
            gram_copy(t).start()

        @pl.when(t >= 1)
        def _():
            for d in range(1, tensors):
                part_copy(t - 1, d).wait()
            summed = part[before]
            for d in range(1, tensors):
                summed = summed + part_in[d - 1, before]
            total[before, own_rows] = summed
            total_copy(t - 1).start()

        @pl.when(t < count)
        def _():
            gram_copy(t).wait()
            part[now] = gram[now, own_rows] + gram_in[now]
            for d in range(1, tensors):
                part_copy(t, d).start()
            relay(t).start()

        @pl.when(t >= 1)
        def _():
            total_copy(t - 1).wait()
            factor_steps(bench, total[before])

            @pl.when(t >= 1 + RING)
            def _():
                out_copy(t - 1 - RING).wait()

            relay(t - 1).wait()

            def columns_of(h, inner):
                source = jnp.where(h == 0, t - 1, rounds + before)
                side = jnp.where(h == 0, island, partner)
                target = pl.ds(pl.multiple_of(side * half, half), half)
                value = scale * product(bench[5], block[source].reshape(size, half))
                final[before, :, target] = value.astype(jnp.bfloat16)
                return inner

            lax.fori_loop(0, 2, columns_of, 0)
            out_copy(t - 1).start()

        return carry

    lax.fori_loop(0, count + 1, run, 0)

    def drain(k, carry):
        out_copy(count - RING + k).wait()
        return carry

    lax.fori_loop(0, RING, drain, 0)

    def finish(r, carry):
        others(r, lambda q, first, peer: row_copy(q, first, peer).wait_send())
        return carry

    lax.fori_loop(0, rounds, finish, 0)


def step(index, own_grad, counts, most, n, tensors, collective_id):
    blocks, rows, columns = own_grad.shape
    half = columns // 2
    size = n * rows
    rounds = max(counts)
    dma = pltpu.SemaphoreType.DMA
    return pl.pallas_call(
        functools.partial(step_kernel, n, tensors, most, counts, math.sqrt(columns * tensors)),
        out_shape=jax.ShapeDtypeStruct((most, size, columns), jnp.bfloat16),
        in_specs=[pl.BlockSpec(memory_space=pltpu.SMEM), pl.BlockSpec(memory_space=pl.ANY)],
        out_specs=pl.BlockSpec(memory_space=pl.ANY),
        scratch_shapes=[
            pltpu.VMEM((blocks, rows, half), jnp.float32),
            pltpu.VMEM((blocks, rows, half), jnp.float32),
            pltpu.VMEM((STAGES, n, rows, half), jnp.float32),
            pltpu.VMEM((rounds, n, rows, half), jnp.float32),
            pltpu.VMEM((rounds + RING, n, rows, half), jnp.float32),
            pltpu.VMEM((6, size, size), jnp.float32),
            pltpu.VMEM((RING, size, size), jnp.float32),
            pltpu.VMEM((RING, size // 2, size), jnp.float32),
            pltpu.VMEM((RING, size // 2, size), jnp.float32),
            pltpu.VMEM((tensors - 1, RING, size // 2, size), jnp.float32),
            pltpu.VMEM((RING, size, size), jnp.float32),
            pltpu.VMEM((RING, size, columns), jnp.bfloat16),
            dma((2, LOADS)),
            dma((STAGES,)),
            dma((rounds,)),
            dma((rounds, n)),
            dma((rounds, n)),
            dma((RING,)),
            dma((RING,)),
            dma((RING,)),
            dma((RING,)),
            dma((RING, tensors)),
            dma((RING, tensors)),
            dma((RING,)),
            dma((RING,)),
            dma((RING,)),
        ],
        compiler_params=pltpu.CompilerParams(
            collective_id=collective_id, has_side_effects=True, vmem_limit_bytes=63 * 2**20
        ),
    )(index, own_grad)


def place_kernel(place_ref, valid_ref, fin_ref, out_ref, held, in_sem, out_sem):
    count = held.shape[0]

    def fetch(s):
        return pltpu.make_async_copy(fin_ref.at[place_ref[s]], held.at[s], in_sem.at[s])

    def store(s):
        return pltpu.make_async_copy(held.at[s], out_ref.at[0, s], out_sem.at[s])

    def begin(s, carry):
        fetch(s).start()
        return carry

    def forward(s, carry):
        fetch(s).wait()

        @pl.when(valid_ref[s] == 0)
        def _():
            held[s] = jnp.zeros(held.shape[1:], held.dtype)

        store(s).start()
        return carry

    def end(s, carry):
        store(s).wait()
        return carry

    lax.fori_loop(0, count, begin, 0)
    lax.fori_loop(0, count, forward, 0)
    lax.fori_loop(0, count, end, 0)


def placed(fin, place, valid):
    count = place.shape[0]
    _, size, columns = fin.shape
    scalars = pl.BlockSpec(memory_space=pltpu.SMEM)
    anywhere = pl.BlockSpec(memory_space=pl.ANY)
    dma = pltpu.SemaphoreType.DMA
    return pl.pallas_call(
        place_kernel,
        in_specs=[scalars, scalars, anywhere],
        out_specs=anywhere,
        out_shape=jax.ShapeDtypeStruct((1, count, size, columns), jnp.bfloat16),
        scratch_shapes=[pltpu.VMEM((count, size, columns), jnp.bfloat16), dma((count,)), dma((count,))],
    )(place, valid, fin)


def table_kernel(n, most, classes, owner_ref, send_ref, place_ref, valid_ref, choice_ref, needed):
    mine = lax.axis_index("island") * n + lax.axis_index("dp")

    def clear(ref):
        def one(i, carry):
            ref[i] = 0
            return carry

        lax.fori_loop(0, ref.shape[0], one, 0)

    for ref in (send_ref, place_ref, valid_ref, needed):
        clear(ref)

    def one(b, held):
        owner = owner_ref[b]
        chip = lax.rem(owner, n)
        slot = needed[chip]
        needed[chip] = slot + 1
        send_ref[chip * most + slot] = b

        @pl.when(owner == mine)
        def _():
            place_ref[held] = slot
            valid_ref[held] = 1

        return held + (owner == mine).astype(jnp.int32)

    lax.fori_loop(0, owner_ref.shape[0], one, jnp.int32(0))
    choice = jnp.int32(len(classes) - 1)
    for k in range(len(classes) - 2, -1, -1):
        fits = needed[0] <= classes[k][0]
        for d in range(1, n):
            fits = fits & (needed[d] <= classes[k][d])
        choice = jnp.where(fits, jnp.int32(k), choice)
    choice_ref[0] = choice


def tables(block_owner, n, most, slot_count, classes):
    scalars = pl.BlockSpec(memory_space=pltpu.SMEM)
    return pl.pallas_call(
        functools.partial(table_kernel, n, most, classes),
        in_specs=[scalars],
        out_specs=(scalars,) * 4,
        out_shape=tuple(jax.ShapeDtypeStruct((c,), jnp.int32) for c in (n * most, slot_count, slot_count, 1)),
        scratch_shapes=[pltpu.SMEM((n,), jnp.int32)],
    )(block_owner)


def cut_load(counts):
    n = len(counts)
    loads = []
    for i in range(1, n):
        loads.append((n - i) * sum(counts[:i]))
        loads.append(i * sum(counts[i:]))
    return max(loads)


PROFILES = (
    (5, 5, 5, 5), (6, 6, 6, 6), (3, 8, 8, 3), (3, 6, 3, 6), (6, 3, 3, 6), (6, 3, 6, 3), (8, 4, 4, 8),
    (3, 6, 6, 3), (5, 6, 5, 6), (6, 5, 6, 5), (3, 5, 3, 5), (3, 5, 5, 3), (4, 8, 8, 4), (5, 3, 3, 5),
)


def count_classes(n, most, least, unit):
    uniform = [(c,) * n for c in range(unit, most + 1, unit) if c >= least]
    shaped = [tuple(unit * k for k in profile) for profile in PROFILES if len(profile) == n]
    shaped = [counts for counts in shaped if max(counts) <= most]
    if shaped:
        uniform = [(most,) * n]
    return sorted(uniform + shaped, key=cut_load)


def body(pseudo_grad, block_owner):
    own_grad = pseudo_grad[0]
    blocks = own_grad.shape[0]
    dp_count = lax.axis_size("dp")
    island_count = lax.axis_size("island")
    tensors = lax.axis_size("tensor")
    owner_count = island_count * dp_count
    slot_count = 2 * (blocks // owner_count)
    most = island_count * slot_count
    classes = count_classes(dp_count, most, blocks // dp_count, max(1, slot_count // 4))
    send_index, place, valid, choice = tables(block_owner, dp_count, most, slot_count, classes)

    def branch(counts, number):
        def run(index, own_grad):
            return step(index, own_grad, counts, most, dp_count, tensors, number)

        return run

    branches = [branch(c, i) for i, c in enumerate(classes)]
    fin = lax.switch(choice[0], branches, send_index, own_grad)
    return placed(fin, place, valid)


def solution(mesh):
    in_specs = (P("island", None, "dp", "tensor"), P())
    out_specs = P(("island", "dp"), None, None, "tensor")
    return jax.shard_map(body, mesh=mesh, in_specs=in_specs, out_specs=out_specs, check_vma=False)
```
